32 devices in a mesh: seq: 8 (over z, x), head: 4 (over y, core).
Axes of the slice: x: 2, y: 2, z: 4, core: 2. Of those that a mesh axis runs over, the one named last changes fastest.
Arguments:
- query: bfloat16 [8192, 4096], P('seq', 'head'), may hold values from -140 to 140
- key: bfloat16 [8192, 512], P('seq'), may hold values from -7 to 7
- value: bfloat16 [8192, 512], P('seq'), may hold values from -6 to 6
- out_grad: bfloat16 [8192, 4096], P('seq', 'head'), may hold values from -6 to 6
- chosen: int32 [32, 16, 4], P('head', 'seq'), may hold values from 0 to 15, as said below
- drop_seed: int32 [32], P('head'), may hold values from 0 to 16777215
Outputs:
- query_grad: float32 [8192, 4096], P('seq', 'head')
- key_grad: float32 [8192, 512], P(('seq', 'head'))
- value_grad: float32 [8192, 512], P(('seq', 'head'))
The draws below stay inside these ranges and needn't reach their ends.
Inputs may be any that keep to these rules, and one draw needn't show every extreme that they name: `chosen`: for head h and query block b, entry 0 is b; the other entries are distinct blocks before b whose shard lies at most 3 shards of 1024 tokens before the shard of b, or b itself where fewer such blocks exist.
All inputs are finite; a program needn't handle non-finite values.
Results may differ from the reference program's by a relative error of at most 0.014.
Values may be sent and summed in bfloat16 or wider, within the bound.
A program may use at most 128 MiB of HBM per device.

```python
import jax
import jax.numpy as jnp
from jax import lax

HD = 128
HEADS = 32
KVH = 4
BLK = 512
TOPK = 4
TOK_DEV = 1024
WIN = 4
SEQ = 8192
NQB = 16


def key_field(key):
    raw = jnp.clip(jax.random.normal(jax.random.fold_in(key, 11), (SEQ, KVH * HD), jnp.float32), -6.0, 6.0)
    return raw


def draw_key(key, part):
    return key_field(key).astype(jnp.bfloat16)


def draw_query(key, part):
    base = jnp.clip(jax.random.normal(jax.random.fold_in(key, 13), (SEQ, HEADS * HD), jnp.float32), -6.0, 6.0)
    return base.astype(jnp.bfloat16)


def draw_chosen(key, part):
    per_shard = TOK_DEV // BLK
    width = WIN * per_shard
    block_ids = jnp.arange(NQB, dtype=jnp.int32)
    lowest = jnp.maximum(0, (block_ids // per_shard - WIN + 1) * per_shard)
    column = jnp.arange(width, dtype=jnp.int32)
    candidate = lowest[:, None] + column[None, :]
    usable = candidate < block_ids[:, None]
    draws = jax.random.randint(jax.random.fold_in(key, 21), (HEADS, NQB, width), 0, 1 << 20, dtype=jnp.int32)
    scores = jnp.where(usable[None], draws * width + column[None, None, :], -1 - column[None, None, :])
    picked_scores, picked_cols = lax.top_k(scores, TOPK - 1)
    picked = lowest[None, :, None] + picked_cols.astype(jnp.int32)
    picked = jnp.where(picked_scores >= 0, picked, block_ids[None, :, None])
    own = jnp.broadcast_to(block_ids[None, :, None], (HEADS, NQB, 1))
    return jnp.concatenate([own, picked], axis=2).astype(jnp.int32)


def with_ends(drawn, rng, low, high):
    index_at = [jax.random.randint(jax.random.fold_in(rng, axis), (), 0, length) for axis, length in enumerate(drawn.shape)]
    main_axis = drawn.shape.index(max(drawn.shape))
    beside = index_at[:main_axis] + [(index_at[main_axis] + 1) % drawn.shape[main_axis]] + index_at[main_axis + 1:]
    return drawn.at[tuple(index_at)].set(low).at[tuple(beside)].set(high)


def shard_levels(rng, shape, pieces, smallest, high):
    factor_of, own = 1.0, jax.random.fold_in(rng, 6)
    for dim, blocks in pieces:
        steps = jnp.exp(jax.random.uniform(jax.random.fold_in(own, dim), (blocks,), jnp.float32, smallest / len(pieces), high / len(pieces)))
        factor_of = factor_of * jnp.repeat(steps, shape[dim] // blocks).reshape([-1 if axis == dim else 1 for axis in range(len(shape))])
    return factor_of


def normal_values(own_key, extent, scale, most, split=(), held_as=jnp.bfloat16):
    gain = shard_levels(own_key, extent, split, -0.22, 0.18) if split else 1.0
    result = jax.random.normal(own_key, extent, jnp.float32) * scale * gain
    return jnp.minimum(jnp.maximum(result, -most), most).astype(held_as)


def setup_inputs(seed: int = 0) -> dict:
    streams_of = jax.random.split(jax.random.key(seed), 7)
    query = draw_query(jax.random.fold_in(streams_of[6], 71), 0)
    key = draw_key(jax.random.fold_in(streams_of[6], 71), 0)
    value = normal_values(streams_of[2], (SEQ, KVH * HD), 1.0, 6.0, ((0, 8),))
    out_grad = normal_values(streams_of[3], (SEQ, HEADS * HD), 1.0, 6.0, ((0, 8), (1, 4)))
    chosen = draw_chosen(jax.random.fold_in(streams_of[6], 71), 0)
    drop_seed = with_ends(jax.random.randint(streams_of[5], (HEADS,), 0, 16777216), jax.random.fold_in(streams_of[5], 1), 0, 16777215).astype(jnp.int32)
    return dict(query=query, key=key, value=value, out_grad=out_grad, chosen=chosen, drop_seed=drop_seed)


drop_cut = 6554
keep_gain = 1.0 / 0.9


def keep_scale(seed_value, query_pos, key_pos):
    mixed = seed_value + query_pos[:, None] * 40503 + key_pos[None, :] * 9973
    mixed = mixed ^ (jnp.right_shift(mixed, 15) & 131071)
    mixed = mixed * 73244475
    mixed = mixed ^ (jnp.right_shift(mixed, 13) & 524287)
    return jnp.where((mixed & 65535) >= drop_cut, keep_gain, 0.0).astype(jnp.float32)


def block_grads(query_block, out_block, key_sel, value_sel, query_pos, key_pos, allowed, seed_value):
    factor = key_sel.shape[-1] ** -0.5
    scores = jnp.dot(query_block, key_sel.T, preferred_element_type=jnp.float32) * factor
    scores = jnp.where(allowed, scores, -jnp.inf)
    peak = jnp.max(scores, axis=1, keepdims=True)
    total = jnp.sum(jnp.exp(scores - peak), axis=1, keepdims=True)
    probs = jnp.exp(scores - (peak + jnp.log(total)))
    gains = keep_scale(seed_value, query_pos, key_pos)
    dropped = (probs * gains).astype(jnp.bfloat16)
    output = jnp.dot(dropped, value_sel, preferred_element_type=jnp.float32)
    delta = jnp.sum(out_block.astype(jnp.float32) * output, axis=1, keepdims=True)
    pgrad = jnp.dot(out_block, value_sel.T, preferred_element_type=jnp.float32)
    sgrad = (probs * (pgrad * gains - delta)).astype(jnp.bfloat16)
    qgrad = jnp.dot(sgrad, key_sel, preferred_element_type=jnp.float32) * factor
    kgrad = jnp.dot(sgrad.T, query_block, preferred_element_type=jnp.float32) * factor
    vgrad = jnp.dot(dropped.T, out_block, preferred_element_type=jnp.float32)
    return qgrad, kgrad, vgrad


def reference(query, key, value, out_grad, chosen, drop_seed):
    seq_len = query.shape[0]
    blocks = seq_len // BLK
    group = HEADS // KVH
    head_list = jnp.repeat(jnp.arange(HEADS, dtype=jnp.int32), blocks)
    block_list = jnp.tile(jnp.arange(blocks, dtype=jnp.int32), HEADS)
    lists = chosen.reshape(HEADS * blocks, TOPK).astype(jnp.int32)
    seeds = jnp.repeat(drop_seed, blocks).astype(jnp.int32)
    offsets = jnp.arange(BLK, dtype=jnp.int32)

    def visit(carry, item):
        key_grad, value_grad = carry
        head, block, picks, seed_value = item
        kv_col = ((head // group) * HD).astype(jnp.int32)
        query_rows = (block * BLK).astype(jnp.int32)
        query_block = lax.dynamic_slice(query, (query_rows, (head * HD).astype(jnp.int32)), (BLK, HD))
        out_block = lax.dynamic_slice(out_grad, (query_rows, (head * HD).astype(jnp.int32)), (BLK, HD))
        key_parts, value_parts, pos_parts, live_parts = [], [], [], []
        for entry in range(TOPK):
            start = (picks[entry] * BLK).astype(jnp.int32)
            key_parts.append(lax.dynamic_slice(key, (start, kv_col), (BLK, HD)))
            value_parts.append(lax.dynamic_slice(value, (start, kv_col), (BLK, HD)))
            pos_parts.append(start + offsets)
            if entry == 0:
                fresh = jnp.ones((BLK,), dtype=bool)
            else:
                fresh = jnp.broadcast_to(jnp.logical_not(jnp.any(picks[:entry] == picks[entry])), (BLK,))
            live_parts.append(fresh)
        key_pos = jnp.concatenate(pos_parts)
        query_pos = query_rows + offsets
        allowed = (key_pos[None, :] <= query_pos[:, None]) & jnp.concatenate(live_parts)[None, :]
        qgrad, kgrad, vgrad = block_grads(query_block, out_block, jnp.concatenate(key_parts), jnp.concatenate(value_parts), query_pos, key_pos, allowed, seed_value)
        for entry in range(TOPK):
            start = (picks[entry] * BLK).astype(jnp.int32)
            old_key = lax.dynamic_slice(key_grad, (start, kv_col), (BLK, HD))
            key_grad = lax.dynamic_update_slice(key_grad, old_key + kgrad[entry * BLK:(entry + 1) * BLK], (start, kv_col))
            old_value = lax.dynamic_slice(value_grad, (start, kv_col), (BLK, HD))
            value_grad = lax.dynamic_update_slice(value_grad, old_value + vgrad[entry * BLK:(entry + 1) * BLK], (start, kv_col))
        return (key_grad, value_grad), qgrad

    empty = jnp.zeros((seq_len, KVH * HD), jnp.float32)
    (key_grad, value_grad), qgrads = lax.scan(visit, (empty, empty), (head_list, block_list, lists, seeds))
    query_grad = qgrads.reshape(HEADS, blocks, BLK, HD).transpose(1, 2, 0, 3).reshape(seq_len, HEADS * HD)
    return query_grad, key_grad, value_grad
```

```python
import math

import jax
import jax.numpy as jnp
from jax import lax
from jax.experimental import pallas as pl
from jax.experimental.pallas import tpu as pltpu
from jax.sharding import PartitionSpec as P

HD = 128
HEADS = 32
KVH = 4
BLK = 512
TOPK = 4
SPAN = 8
SUB = 128
ROWS = 16

drop_cut = 6554
keep_gain = 1.0 / 0.9
factor = HD ** (-0.5)
exp_scale = factor * math.log2(math.e)


def shifted(array, axis, by):
    size = lax.axis_size(axis)
    pairs = [(i, i + by) for i in range(size) if 0 <= i + by < size]
    return lax.ppermute(array, axis, pairs)


def kept(x):
    x = x ^ lax.shift_right_logical(x, 15)
    x = x * 73244475
    x = x ^ lax.shift_right_logical(x, 13)
    return (x & 65535) >= drop_cut


def dot(a, b):
    return jnp.dot(a, b, preferred_element_type=jnp.float32)


def grads_kernel(local_blocks, window, steps, chosen_ref, seed_ref, q_hbm, do_hbm, key_ref, value_ref, gathered_ref,
                 bits_hbm, qg_ref, far_ref, own_ref, s0, s1, g0, g1, d0, d1, sg0, sg1, mx0, mx1, qt0, qt1, dt0, dt1,
                 qn0, qn1, dn0, dn1, inv0, inv1, out0, out1, acc_ref, kt_ref, kv_ref, bits_ref, q_ref, do_ref,
                 load_sem, out_sem):
    S, G, D, SG = (s0, s1), (g0, g1), (d0, d1), (sg0, sg1)
    MX, QT, DT = (mx0, mx1), (qt0, qt1), (dt0, dt1)
    QN, DN, INV, OUT = (qn0, qn1), (dn0, dn1), (inv0, inv1), (out0, out1)
    pair = pl.program_id(0)
    shard = lax.axis_index("seq")
    corner = (lax.broadcasted_iota(jnp.int32, (SUB, SUB), 0)
              <= lax.broadcasted_iota(jnp.int32, (SUB, SUB), 1))

    def picks_of(item):
        return [chosen_ref[item * TOPK + t] for t in range(TOPK)]

    def place(pick):
        return shard - pick // local_blocks, pl.multiple_of(lax.rem(pick, local_blocks) * BLK, BLK)

    def where_of(item):
        head = item // local_blocks
        return (pl.ds(pl.multiple_of(lax.rem(item, local_blocks) * BLK, BLK), BLK),
                pl.ds(pl.multiple_of(head * HD, HD), HD))

    def low(t, row):
        return row // SUB * SUB if t == 0 else 0

    def score_parts(item, p):
        places = [place(pick) for pick in picks_of(item)]

        def turn():
            rows, cols = where_of(item)
            QT[p][...] = q_ref[rows, cols].T
            DT[p][...] = do_ref[rows, cols].T

        def scores(t, row, size):
            slot, within = places[t]
            lo = low(t, row)
            keys = kv_ref[slot, 0, pl.ds(within + row, size), :]
            s = dot(keys, QT[p][:, lo:])
            if t == 0:
                edge = jnp.where(corner, s[:, :SUB], -jnp.inf)
                s = edge if lo + SUB == BLK else jnp.concatenate([edge, s[:, SUB:]], axis=1)
            S[p][t * BLK + row:t * BLK + row + size, lo:] = s
            top = jnp.max(s.reshape(size // 8, 8, BLK - lo), axis=0)
            if row:
                top = jnp.maximum(MX[p][t, :, lo:], top)
            MX[p][t, :, lo:] = top

        def pulls(t, row, size):
            slot, within = places[t]
            lo = low(t, row)
            values = kv_ref[slot, 1, pl.ds(within + row, size), :]
            G[p][t * BLK + row:t * BLK + row + size, lo:] = dot(values, DT[p][:, lo:])

        parts = [turn]
        for t in range(TOPK):
            size = SUB if t == 0 else 2 * SUB
            for row in range(0, BLK, size):
                parts.append(lambda t=t, row=row, size=size: scores(t, row, size))
                parts.append(lambda t=t, row=row, size=size: pulls(t, row, size))
        return parts

    def soft_parts(item, p):
        picks = picks_of(item)
        live = [None]
        for t in range(1, TOPK):
            dead = picks[t] == picks[0]
            for u in range(1, t):
                dead = jnp.logical_or(dead, picks[t] == picks[u])
            live.append(jnp.logical_not(dead))
        st = {}

        def head():
            tops = MX[p][0]
            for t in range(1, TOPK):
                tops = jnp.maximum(tops, jnp.where(live[t], MX[p][t], -jnp.inf))
            peak = jnp.max(tops, axis=0, keepdims=True) * exp_scale
            st["base"] = [peak] + [jnp.where(live[t], peak, 3e38) for t in range(1, TOPK)]
            st["total"] = jnp.zeros((8, BLK), jnp.float32)
            st["delta"] = jnp.zeros((8, BLK), jnp.float32)

        word = item * TOPK // 32

        def weigh(t, row):
            lo = low(t, row)
            at = (slice(t * BLK + row, t * BLK + row + ROWS), slice(lo, BLK))
            bit = lax.shift_left(jnp.int32(1), lax.rem(item * TOPK, 32) + t)
            keep = (bits_ref[word, row:row + ROWS, lo:] & bit) != 0
            e = jnp.exp2(S[p][at] * exp_scale - st["base"][t][:, lo:])
            d = jnp.where(keep, e, 0.0)
            dp = d * G[p][at]
            S[p][at] = e
            G[p][at] = dp
            D[p][at] = d.astype(jnp.bfloat16)
            wide = BLK - lo
            e_sum = jnp.sum(e.reshape(ROWS // 8, 8, wide), axis=0)
            dp_sum = jnp.sum(dp.reshape(ROWS // 8, 8, wide), axis=0)
            if lo:
                pad = lambda old, add: jnp.concatenate([old[:, :lo], old[:, lo:] + add], axis=1)
            else:
                pad = lambda old, add: old + add
            st["total"] = pad(st["total"], e_sum)
            st["delta"] = pad(st["delta"], dp_sum)

        def middle():
            inv = 1.0 / jnp.sum(st["total"], axis=0, keepdims=True)
            st["mean"] = jnp.sum(st["delta"], axis=0, keepdims=True) * inv
            INV[p][...] = inv
            QN[p][...] = (QT[p][...].astype(jnp.float32) * inv).astype(jnp.bfloat16)
            DN[p][...] = (DT[p][...].astype(jnp.float32) * inv).astype(jnp.bfloat16)

        def slope(t, row):
            lo = low(t, row)
            at = (slice(t * BLK + row, t * BLK + row + ROWS), slice(lo, BLK))
            SG[p][at] = (G[p][at] - S[p][at] * st["mean"][:, lo:]).astype(jnp.bfloat16)

        parts = [(1, head)]
        spots = [(t, row) for t in range(TOPK) for row in range(0, BLK, ROWS)]
        for t, row in spots:
            parts.append((3, lambda t=t, row=row: weigh(t, row)))
        parts.append((1, middle))
        for t, row in spots:
            parts.append((1, lambda t=t, row=row: slope(t, row)))
        return parts

    def grad_parts(item, p):
        places = [place(pick) for pick in picks_of(item)]

        def keyed(t, part):
            slot, within = places[t]
            left, right = ((QN, SG), (DN, D))[part]
            add = lax.dot_general(left[p][...], right[p][t * BLK:(t + 1) * BLK, :], (((1,), (1,)), ((), ())),
                                  preferred_element_type=jnp.float32)
            acc_ref[slot, part, :, pl.ds(within, BLK)] += add

        def queried(lo, size):
            keys_t = jnp.concatenate([kt_ref[slot, :, pl.ds(within, BLK)] for slot, within in places], axis=1)
            part = dot(keys_t, SG[p][:, lo:lo + size])
            OUT[p][lo:lo + size, :] = (part * (INV[p][:, lo:lo + size] * (keep_gain * factor))).T

        parts = []
        for t in range(TOPK):
            parts.append(lambda t=t: keyed(t, 1))
            parts.append(lambda t=t: keyed(t, 0))
            if t % 2:
                parts.append(lambda t=t: queried(t // 2 * 2 * SUB, 2 * SUB))
        return parts

    def run(parts):
        for part in parts:
            part()

    def mix(soft, dots):
        whole = sum(cost for cost, _ in soft)
        done, k = 0, 0
        for cost, part in soft:
            while k < len(dots) and k * whole <= done * len(dots):
                dots[k]()
                k += 1
            part()
            done += cost
        run(dots[k:])

    def weave(a, b):
        spots = [((i + 0.5) / len(a), 0, x) for i, x in enumerate(a)]
        spots += [((i + 0.5) / len(b), 1, x) for i, x in enumerate(b)]
        return [x for _, _, x in sorted(spots, key=lambda y: y[:2])]

    def send(item, p):
        rows, cols = where_of(item)
        return pltpu.make_async_copy(OUT[p], qg_ref.at[rows, cols], out_sem.at[p])

    @pl.when(pair == 0)
    def _():
        kv_col = pl.ds(pl.multiple_of(kv_column(), HD), HD)
        loads = [
            pltpu.make_async_copy(q_hbm, q_ref, load_sem.at[0]),
            pltpu.make_async_copy(do_hbm, do_ref, load_sem.at[1]),
            pltpu.make_async_copy(key_ref.at[:, kv_col], kv_ref.at[0, 0], load_sem.at[2]),
            pltpu.make_async_copy(value_ref.at[:, kv_col], kv_ref.at[0, 1], load_sem.at[3]),
            pltpu.make_async_copy(gathered_ref, kv_ref.at[pl.ds(1, window - 1)], load_sem.at[4]),
            pltpu.make_async_copy(bits_hbm, bits_ref, load_sem.at[5]),
        ]
        for load in loads:
            load.start()
        acc_ref[...] = jnp.zeros_like(acc_ref)
        for ref in D + SG:
            ref[...] = jnp.zeros_like(ref)
        QN[1][...] = jnp.zeros_like(QN[1])
        DN[1][...] = jnp.zeros_like(DN[1])
        INV[1][...] = jnp.zeros_like(INV[1])
        for load in loads:
            load.wait()
        for slot in range(window):
            kt_ref[slot] = kv_ref[slot, 0].T
        run(score_parts(0, 0))

    last = pl.num_programs(0) - 1
    for p in range(2):
        item = pair * 2 + p
        after = jnp.minimum(item + 1, steps - 1)
        before = jnp.maximum(item - 1, 0)
        target = jnp.where(item == 0, 1, item - 1)

        @pl.when(pair > 0)
        def _():
            send(jnp.maximum(target - 2, 0), 1 - p).wait()

        if p == 1:
            pass
        mix(soft_parts(item, p), weave(score_parts(after, 1 - p), grad_parts(before, 1 - p)))
        send(target, 1 - p).start()

    @pl.when(pair == last)
    def _():
        send(0, 1).wait()
        run(grad_parts(steps - 1, 1))
        send(steps - 1, 1).start()
        for part, scale in ((0, keep_gain * factor), (1, keep_gain)):
            own_ref[part] = acc_ref[0, part] * scale
            for slot in range(1, window):
                far_ref[slot - 1, part] = (acc_ref[slot, part] * scale).astype(jnp.bfloat16)
        send(0, 0).wait()
        send(0, 1).wait()


def kv_column():
    return lax.axis_index("head") * (HEADS // lax.axis_size("head")) // (HEADS // KVH) * HD


def block_grads(query, out_grad, key, value, gathered, bits, chosen, drop_seed):
    rows = query.shape[0]
    local_heads = query.shape[1] // HD
    local_blocks = rows // BLK
    window = gathered.shape[0] + 1
    steps = local_heads * local_blocks
    flops = steps * TOPK * 5 * 2 * BLK * BLK * HD
    kernel = lambda *refs: grads_kernel(local_blocks, window, steps, *refs)
    f32, bf16 = jnp.float32, jnp.bfloat16
    twice = lambda shape, dtype: [pltpu.VMEM(shape, dtype)] * 2
    return pl.pallas_call(
        kernel,
        name="block_grads",
        grid_spec=pltpu.PrefetchScalarGridSpec(
            num_scalar_prefetch=2,
            grid=(steps // 2,),
            in_specs=[pl.BlockSpec(memory_space=pl.ANY)] * 6,
            out_specs=[
                pl.BlockSpec(memory_space=pl.ANY),
                pl.BlockSpec((window - 1, 2, HD, rows), lambda i, *_: (0, 0, 0, 0)),
                pl.BlockSpec((2, HD, rows), lambda i, *_: (0, 0, 0)),
            ],
            scratch_shapes=twice((TOPK * BLK, BLK), f32) + twice((TOPK * BLK, BLK), f32)
            + twice((TOPK * BLK, BLK), bf16) + twice((TOPK * BLK, BLK), bf16)
            + twice((TOPK, 8, BLK), f32)
            + twice((HD, BLK), bf16) * 4
            + twice((1, BLK), f32) + twice((BLK, HD), f32)
            + [
                pltpu.VMEM((window, 2, HD, rows), f32),
                pltpu.VMEM((window, HD, rows), bf16),
                pltpu.VMEM((window, 2, rows, HD), bf16),
                pltpu.VMEM(bits.shape, jnp.int32),
                pltpu.VMEM(query.shape, bf16),
                pltpu.VMEM(query.shape, bf16),
                pltpu.SemaphoreType.DMA((6,)),
                pltpu.SemaphoreType.DMA((2,)),
            ],
        ),
        out_shape=[
            jax.ShapeDtypeStruct((rows, local_heads * HD), f32),
            jax.ShapeDtypeStruct((window - 1, 2, HD, rows), bf16),
            jax.ShapeDtypeStruct((2, HD, rows), f32),
        ],
        compiler_params=pltpu.CompilerParams(vmem_limit_bytes=60 << 20),
        cost_estimate=pl.CostEstimate(flops=flops, bytes_accessed=20 << 20, transcendentals=steps * TOPK * BLK * BLK),
    )(chosen.reshape(-1), drop_seed, query, out_grad, key, value, gathered, bits)


def mask_rows(chosen_ref, seed_ref, bits_ref, steps, local_blocks, row, lo):
    shard = lax.axis_index("seq")
    size = 16
    at = (pl.ds(row, size), slice(0, BLK))
    place = ((lax.broadcasted_iota(jnp.int32, (size, BLK), 0) + row) * 9973
             + lax.broadcasted_iota(jnp.int32, (size, BLK), 1) * 40503)
    for word in range(bits_ref.shape[0]):
        held = jnp.zeros((size, BLK), jnp.int32)
        for j in range(32):
            item, t = (word * 32 + j) // TOPK, j % TOPK
            own = shard * local_blocks + item % local_blocks
            base = seed_ref[item // local_blocks] + own * (BLK * 40503) + chosen_ref[item * TOPK + t] * (BLK * 9973)
            cut = lo if t == 0 else 0
            bit = jnp.int32(1 << j if j < 31 else -(1 << 31))
            part = jnp.where(kept(place[:, cut:] + base), bit, 0)
            if cut:
                part = jnp.concatenate([jnp.zeros((size, cut), jnp.int32), part], axis=1)
            held = held | part
        bits_ref[(word,) + at] = held


def masks_kernel(steps, local_blocks, chosen_ref, seed_ref, bits_ref):
    @pl.loop(0, BLK // 16)
    def _(i):
        mask_rows(chosen_ref, seed_ref, bits_ref, steps, local_blocks, pl.multiple_of(i * 16, 16), 0)


def masks(chosen, drop_seed, local_blocks):
    steps = chosen.size // TOPK
    smem = pl.BlockSpec(memory_space=pltpu.SMEM)
    return pl.pallas_call(
        lambda *refs: masks_kernel(steps, local_blocks, *refs),
        name="masks",
        out_shape=jax.ShapeDtypeStruct((steps * TOPK // 32, BLK, BLK), jnp.int32),
        in_specs=[smem, smem],
        out_specs=pl.BlockSpec(memory_space=pltpu.VMEM),
    )(chosen.reshape(-1), drop_seed)


CHUNKS = 4


def seq_peer(by):
    size = lax.axis_size("seq")
    return {"seq": lax.rem(lax.axis_index("seq") + by + size, size)}


def meet(peers):
    barrier = pltpu.get_barrier_semaphore()
    for peer in peers:
        pl.semaphore_signal(barrier, inc=1, device_id=peer, device_id_type=pl.DeviceIdType.MESH)
    pl.semaphore_wait(barrier, len(peers))


def remote(src, dst, send, recv, peer):
    return pltpu.make_async_remote_copy(
        src_ref=src, dst_ref=dst, send_sem=send, recv_sem=recv, device_id=peer,
        device_id_type=pl.DeviceIdType.MESH,
    )


def gather_kernel(steps, local_blocks, chosen_ref, seed_ref, key_ref, value_ref, far_ref, bits_ref, send_sem, recv_sem):
    shard = lax.axis_index("seq")
    size = lax.axis_size("seq")
    odd = lax.rem(shard, 2)
    col = pl.ds(pl.multiple_of(lax.axis_index("head") * HD, HD), HD)
    half = key_ref.shape[0] // 2
    mate = {"seq": shard + 1 - 2 * odd}
    ahead = seq_peer(2)
    barrier = pltpu.get_barrier_semaphore()
    gives = shard < size - 2
    takes = shard >= 2
    relays = jnp.logical_and(odd == 0, jnp.logical_and(gives, takes))
    relayed = jnp.logical_and(odd == 0, shard >= 4)

    def greet(peer):
        pl.semaphore_signal(barrier, inc=1, device_id=peer, device_id_type=pl.DeviceIdType.MESH)

    for peer in (ahead, seq_peer(-2), mate):
        greet(peer)
    pl.semaphore_wait(barrier, 3)

    def own(c):
        return (key_ref, value_ref)[c // 2].at[pl.ds(c % 2 * half, half), col]

    def far(k, c):
        return far_ref.at[k, c // 2, pl.ds(c % 2 * half, half), :]

    def own_ahead(c):
        return remote(own(c), far(1, c), send_sem.at[0, c], recv_sem.at[1, c], ahead)

    def own_mate(c):
        return remote(own(c), far(0, c), send_sem.at[1, c], recv_sem.at[0, c], mate)

    def pass_mate(c, k):
        return remote(far(1, c), far(k, c), send_sem.at[2, c], recv_sem.at[k, c], mate)

    def pass_ahead(c):
        return remote(far(0, c), far(2, c), send_sem.at[3, c], recv_sem.at[2, c], ahead)

    for c in range(CHUNKS):
        @pl.when(gives)
        def _():
            own_ahead(c).start()

        @pl.when(odd == 0)
        def _():
            own_mate(c).start()

    def near_event(c):
        @pl.when(takes)
        def _():
            own_ahead(c).wait_recv()

            @pl.when(odd == 0)
            def _():
                pass_mate(c, 2).start()

            @pl.when(odd == 1)
            def _():
                pass_mate(c, 0).start()

    def far_event(c):
        @pl.when(relays)
        def _():
            own_mate(c).wait_recv()
            pass_ahead(c).start()

    events = [lambda c=c: near_event(c) for c in range(CHUNKS)] + [lambda c=c: far_event(c) for c in range(CHUNKS)]
    order = [0, 1, 4, 2, 5, 3, 6, 7]
    spots = MASK_SPOTS
    rows = 16
    loops = SUB // rows
    for c in range(BLK // SUB):
        @pl.loop(0, loops)
        def _(i):
            for spot, event in zip(spots, order):
                if spot // loops == c:
                    pl.when(i == spot % loops)(events[event])
            mask_rows(chosen_ref, seed_ref, bits_ref, steps, local_blocks,
                      pl.multiple_of(c * SUB + i * rows, rows), c * SUB)

    for c in range(CHUNKS):
        @pl.when(jnp.logical_and(odd == 0, takes))
        def _():
            pass_mate(c, 2).wait_send()

        @pl.when(jnp.logical_and(odd == 0, jnp.logical_and(takes, jnp.logical_not(gives))))
        def _():
            own_mate(c).wait_recv()

        @pl.when(odd == 0)
        def _():
            own_mate(c).wait_send()

        @pl.when(relayed)
        def _():
            pass_ahead(c).wait_recv()

        @pl.when(relays)
        def _():
            pass_ahead(c).wait_send()

        @pl.when(odd == 1)
        def _():
            own_mate(c).wait_recv()

        @pl.when(jnp.logical_and(odd == 1, takes))
        def _():
            remote(far(1, c), far(2, c), send_sem.at[2, c], recv_sem.at[2, c], mate).wait_recv()
            pass_mate(c, 0).wait_send()

        @pl.when(gives)
        def _():
            own_ahead(c).wait_send()


MASK_SPOTS = [11, 14, 15, 18, 19, 22, 23, 27]


def gather(key, value, chosen, drop_seed):
    rows = key.shape[0]
    steps = chosen.size // TOPK
    smem = pl.BlockSpec(memory_space=pltpu.SMEM)
    return pl.pallas_call(
        lambda *refs: gather_kernel(steps, rows // BLK, *refs),
        name="gather",
        out_shape=[
            jax.ShapeDtypeStruct((3, 2, rows, HD), jnp.bfloat16),
            jax.ShapeDtypeStruct((steps * TOPK // 32, BLK, BLK), jnp.int32),
        ],
        in_specs=[smem, smem] + [pl.BlockSpec(memory_space=pl.ANY)] * 2,
        out_specs=[pl.BlockSpec(memory_space=pl.ANY), pl.BlockSpec(memory_space=pltpu.VMEM)],
        scratch_shapes=[pltpu.SemaphoreType.DMA((4, CHUNKS)), pltpu.SemaphoreType.DMA((3, CHUNKS))],
        compiler_params=pltpu.CompilerParams(collective_id=0, has_side_effects=True, vmem_limit_bytes=16 << 20),
    )(chosen.reshape(-1), drop_seed, key, value)


def reduce_kernel(ranks, far_ref, own_ref, kg_ref, vg_ref, in_far, in_near, in_two, in_own, up_near, up_two,
                  in_head, up_head, total, send_sem, recv_sem, head_send, head_recv):
    shard = lax.axis_index("seq")
    rank = lax.axis_index("head")
    odd = lax.rem(shard, 2)
    mate = {"seq": shard + 1 - 2 * odd}
    back = seq_peer(-2)
    others = [{"head": lax.rem(rank + d, ranks)} for d in range(1, ranks)]
    meet([back, seq_peer(2), mate] + others)
    piece = in_near.shape[3]

    def rows(c):
        return pl.ds(c * piece, piece)

    def far_back(c):
        return remote(far_ref.at[2, :, :, rows(c)], in_far.at[c], send_sem.at[0, c], recv_sem.at[0, c], back)

    def own_mate(c):
        return remote(far_ref.at[0, :, :, rows(c)], in_own.at[c], send_sem.at[0, c], recv_sem.at[1, c], mate)

    def far_mate(c):
        return remote(far_ref.at[2, :, :, rows(c)], in_near.at[c], send_sem.at[1, c], recv_sem.at[2, c], mate)

    def near_mate(c):
        return remote(up_near.at[c], in_near.at[c], send_sem.at[1, c], recv_sem.at[2, c], mate)

    def two_back(c):
        return remote(up_two.at[c], in_two.at[c], send_sem.at[2, c], recv_sem.at[3, c], back)

    def to_head(c):
        return remote(up_head.at[c], in_head.at[rank], head_send.at[c], head_recv.at[rank], {"head": c})

    for c in range(ranks):
        @pl.when(odd == 0)
        def _():
            far_back(c).start()

        @pl.when(odd == 1)
        def _():
            far_mate(c).start()

    @pl.when(odd == 1)
    def _():
        for c in range(ranks):
            own_mate(c).start()

    def stage_near(c):
        @pl.when(odd == 0)
        def _():
            far_back(c).wait_recv()
            up_near[c] = (far_ref[0, :, :, rows(c)].astype(jnp.float32) + in_far[c].astype(jnp.float32)).astype(jnp.bfloat16)
            near_mate(c).start()

    def stage_two(c):
        near_mate(c).wait_recv()
        up_two[c] = (far_ref[1, :, :, rows(c)].astype(jnp.float32) + in_near[c].astype(jnp.float32)).astype(jnp.bfloat16)
        two_back(c).start()

    def stage_own(c):
        two_back(c).wait_recv()
        total[c] = own_ref[:, :, rows(c)] + in_two[c].astype(jnp.float32)

        @pl.when(odd == 0)
        def _():
            own_mate(c).wait_recv()
            total[c] += in_own[c].astype(jnp.float32)

        @pl.when(rank == c)
        def _():
            kg_ref[:, c * HD:(c + 1) * HD] = total[c, 0].T
            vg_ref[:, c * HD:(c + 1) * HD] = total[c, 1].T

        @pl.when(rank != c)
        def _():
            up_head[c] = total[c].astype(jnp.bfloat16)
            to_head(c).start()

    for k in range(ranks + 2):
        if k < ranks:
            stage_near(k)
        if 0 <= k - 1 < ranks:
            stage_two(k - 1)
        if 0 <= k - 2:
            stage_own(k - 2)

    for c in range(ranks):
        @pl.when(rank != c)
        def _():
            remote(up_head.at[c], in_head.at[c], head_send.at[c], head_recv.at[c], {"head": c}).wait_recv()
            kg_ref[:, c * HD:(c + 1) * HD] = in_head[c, 0].astype(jnp.float32).T
            vg_ref[:, c * HD:(c + 1) * HD] = in_head[c, 1].astype(jnp.float32).T
            to_head(c).wait_send()

        two_back(c).wait_send()

        @pl.when(odd == 0)
        def _():
            far_back(c).wait_send()
            near_mate(c).wait_send()

        @pl.when(odd == 1)
        def _():
            own_mate(c).wait_send()
            far_mate(c).wait_send()


def reduce(far, own):
    ranks = lax.axis_size("head")
    rows = own.shape[2]
    piece = rows // ranks
    part = pltpu.VMEM((ranks, 2, HD, piece), jnp.bfloat16)
    return pl.pallas_call(
        lambda *refs: reduce_kernel(ranks, *refs),
        name="reduce",
        out_shape=[jax.ShapeDtypeStruct((piece, ranks * HD), jnp.float32)] * 2,
        in_specs=[pl.BlockSpec(memory_space=pltpu.VMEM)] * 2,
        out_specs=[pl.BlockSpec(memory_space=pltpu.VMEM)] * 2,
        scratch_shapes=[part] * 8 + [
            pltpu.VMEM((ranks, 2, HD, piece), jnp.float32),
            pltpu.SemaphoreType.DMA((3, ranks)),
            pltpu.SemaphoreType.DMA((4, ranks)),
            pltpu.SemaphoreType.DMA((ranks,)),
            pltpu.SemaphoreType.DMA((ranks,)),
        ],
        compiler_params=pltpu.CompilerParams(collective_id=1, has_side_effects=True, vmem_limit_bytes=32 << 20),
    )(far, own)


def local(query, key, value, out_grad, chosen, drop_seed):
    rows = query.shape[0]
    local_heads = query.shape[1] // HD
    size = lax.axis_size("seq")
    ranks = lax.axis_size("head")
    window = min(SPAN, size // 2)
    kv_col = kv_column()
    paired = window == 4 and ranks == KVH and size % 2 == 0
    if paired:
        gathered, bits = gather(key, value, chosen, drop_seed)
    else:
        bits = masks(chosen, drop_seed, rows // BLK)
        own_pair = jnp.stack(
            [
                lax.dynamic_slice_in_dim(key, kv_col, HD, 1),
                lax.dynamic_slice_in_dim(value, kv_col, HD, 1),
            ]
        )
        gathered = jnp.stack([shifted(own_pair, "seq", d) for d in range(1, window)])
    query_grad, far, own = block_grads(query, out_grad, key, value, gathered, bits, chosen, drop_seed)
    if paired:
        key_grad, value_grad = reduce(far, own)
        return (query_grad, key_grad, value_grad)
    for d in range(1, window):
        own = own + shifted(far[d - 1], "seq", -d).astype(jnp.float32)
    pieces = own.transpose(0, 2, 1).reshape(2, ranks, rows // ranks, HD)
    swapped = lax.all_to_all(pieces, "head", 1, 1, tiled=True)
    summed = swapped.reshape(2, KVH, ranks // KVH, rows // ranks, HD).sum(2)
    both = summed.transpose(0, 2, 1, 3).reshape(2, rows // ranks, KVH * HD)
    return (query_grad, both[0], both[1])


def solution(mesh):
    in_specs = (
        P("seq", "head"),
        P("seq", None),
        P("seq", None),
        P("seq", "head"),
        P("head", "seq", None),
        P("head"),
    )
    out_specs = (P("seq", "head"), P(("seq", "head"), None), P(("seq", "head"), None))
    return jax.shard_map(local, mesh=mesh, in_specs=in_specs, out_specs=out_specs, check_vma=False)
```

```python
import math

import jax
import jax.numpy as jnp
from jax import lax
from jax.experimental import pallas as pl
from jax.experimental.pallas import tpu as pltpu
from jax.sharding import PartitionSpec as P

HD = 128
HEADS = 32
KVH = 4
BLK = 512
TOPK = 4
SPAN = 8
SUB = 128
ROWS = 16
PIECE = 128
LAG = 1

drop_cut = 6554
keep_gain = 1.0 / 0.9
factor = HD ** (-0.5)
exp_scale = factor * math.log2(math.e)


def shifted(array, axis, by):
    size = lax.axis_size(axis)
    pairs = [(i, i + by) for i in range(size) if 0 <= i + by < size]
    return lax.ppermute(array, axis, pairs)


def kept(x):
    x = x ^ lax.shift_right_logical(x, 15)
    x = x * 73244475
    x = x ^ lax.shift_right_logical(x, 13)
    return (x & 65535) >= drop_cut


def dot(a, b):
    return jnp.dot(a, b, preferred_element_type=jnp.float32)


def grads_kernel(local_blocks, window, steps, chosen_ref, seed_ref, q_hbm, do_hbm, key_ref, value_ref, gathered_ref,
                 bits_hbm, qg_ref, far_ref, own_ref, s0, s1, g0, g1, d0, d1, sg0, sg1, mx0, mx1, qt0, qt1, dt0, dt1,
                 qn0, qn1, dn0, dn1, inv0, inv1, out0, out1, acc_ref, kt_ref, kv_ref, bits_ref, q_ref, do_ref,
                 load_sem, out_sem):
    S, G, D, SG = (s0, s1), (g0, g1), (d0, d1), (sg0, sg1)
    MX, QT, DT = (mx0, mx1), (qt0, qt1), (dt0, dt1)
    QN, DN, INV, OUT = (qn0, qn1), (dn0, dn1), (inv0, inv1), (out0, out1)
    pair = pl.program_id(0)
    shard = lax.axis_index("seq")
    corner = (lax.broadcasted_iota(jnp.int32, (SUB, SUB), 0)
              <= lax.broadcasted_iota(jnp.int32, (SUB, SUB), 1))

    def picks_of(item):
        return [chosen_ref[item * TOPK + t] for t in range(TOPK)]

    def place(pick):
        return shard - pick // local_blocks, pl.multiple_of(lax.rem(pick, local_blocks) * BLK, BLK)

    def where_of(item):
        head = item // local_blocks
        return (pl.ds(pl.multiple_of(lax.rem(item, local_blocks) * BLK, BLK), BLK),
                pl.ds(pl.multiple_of(head * HD, HD), HD))

    def low(t, row):
        return row // SUB * SUB if t == 0 else 0

    def spread(x):
        zero = jnp.maximum(jnp.minimum(x[-8:, :], 0.0), 0.0)
        wide = zero.shape[1]
        return jnp.concatenate([zero] * (BLK // wide) + ([zero[:, :BLK % wide]] if BLK % wide else []), axis=1)

    def score_parts(item, p):
        places = [place(pick) for pick in picks_of(item)]

        def turn():
            rows, cols = where_of(item)
            QT[p][...] = q_ref[rows, cols].T
            DT[p][...] = do_ref[rows, cols].T

        def scores(t, row, size):
            slot, within = places[t]
            lo = low(t, row)
            keys = kv_ref[slot, 0, pl.ds(within + row, size), :]
            s = dot(keys, QT[p][:, lo:])
            tie = spread(s)
            if t == 0:
                edge = jnp.where(corner, s[:, :SUB], -jnp.inf)
                s = edge if lo + SUB == BLK else jnp.concatenate([edge, s[:, SUB:]], axis=1)
            S[p][t * BLK + row:t * BLK + row + size, lo:] = s
            top = jnp.max(s.reshape(size // 8, 8, BLK - lo), axis=0)
            if row:
                top = jnp.maximum(MX[p][t, :, lo:], top)
            MX[p][t, :, lo:] = top
            return tie

        def pulls(t, row, size):
            slot, within = places[t]
            lo = low(t, row)
            values = kv_ref[slot, 1, pl.ds(within + row, size), :]
            g = dot(values, DT[p][:, lo:])
            G[p][t * BLK + row:t * BLK + row + size, lo:] = g
            return spread(g)

        parts = [turn]
        for t in range(TOPK):
            size = SUB if t == 0 else PIECE
            for row in range(0, BLK, size):
                parts.append(lambda t=t, row=row, size=size: scores(t, row, size))
                parts.append(lambda t=t, row=row, size=size: pulls(t, row, size))
        return parts

    def soft_parts(item, p, ties):
        picks = picks_of(item)
        live = [None]
        for t in range(1, TOPK):
            dead = picks[t] == picks[0]
            for u in range(1, t):
                dead = jnp.logical_or(dead, picks[t] == picks[u])
            live.append(jnp.logical_not(dead))
        st = {}

        def head():
            tops = MX[p][0]
            for t in range(1, TOPK):
                tops = jnp.maximum(tops, jnp.where(live[t], MX[p][t], -jnp.inf))
            peak = jnp.max(tops, axis=0, keepdims=True) * exp_scale
            peak = jnp.broadcast_to(peak, (8, BLK))
            st["base"] = [peak] + [jnp.where(live[t], peak, 3e38) for t in range(1, TOPK)]
            st["total"] = jnp.zeros((8, BLK), jnp.float32)
            st["delta"] = jnp.zeros((8, BLK), jnp.float32)

        word = item * TOPK // 32

        def weigh(t, row):
            lo = low(t, row)
            at = (slice(t * BLK + row, t * BLK + row + ROWS), slice(lo, BLK))
            bit = lax.shift_left(jnp.int32(1), lax.rem(item * TOPK, 32) + t)
            keep = (bits_ref[word, row:row + ROWS, lo:] & bit) != 0
            wide = BLK - lo
            base = st["base"][t][:, lo:]
            if ties:
                base = base + ties.pop()[:, lo:]
                st["base"][t] = base if not lo else jnp.concatenate([st["base"][t][:, :lo], base], axis=1)
            scaled = (S[p][at] * exp_scale).reshape(ROWS // 8, 8, wide) - base[None]
            e = jnp.exp2(scaled.reshape(ROWS, wide))
            d = jnp.where(keep, e, 0.0)
            dp = d * G[p][at]
            S[p][at] = e
            G[p][at] = dp
            D[p][at] = d.astype(jnp.bfloat16)
            e_sum = jnp.sum(e.reshape(ROWS // 8, 8, wide), axis=0)
            dp_sum = jnp.sum(dp.reshape(ROWS // 8, 8, wide), axis=0)
            if lo:
                pad = lambda old, add: jnp.concatenate([old[:, :lo], old[:, lo:] + add], axis=1)
            else:
                pad = lambda old, add: old + add
            st["total"] = pad(st["total"], e_sum)
            st["delta"] = pad(st["delta"], dp_sum)

        def middle():
            inv = 1.0 / jnp.sum(st["total"], axis=0, keepdims=True)
            st["mean"] = jnp.broadcast_to(jnp.sum(st["delta"], axis=0, keepdims=True) * inv, (8, BLK))
            INV[p][...] = inv
            QN[p][...] = (QT[p][...].astype(jnp.float32) * inv).astype(jnp.bfloat16).T
            DN[p][...] = (DT[p][...].astype(jnp.float32) * inv).astype(jnp.bfloat16).T

        def slope(t, row):
            lo = low(t, row)
            at = (slice(t * BLK + row, t * BLK + row + ROWS), slice(lo, BLK))
            if ties:
                st["mean"] = st["mean"] + ties.pop()
            wide = BLK - lo
            less = S[p][at].reshape(ROWS // 8, 8, wide) * st["mean"][None, :, lo:]
            SG[p][at] = (G[p][at] - less.reshape(ROWS, wide)).astype(jnp.bfloat16)

        parts = [(1, head)]
        spots = [(t, row) for t in range(TOPK) for row in range(0, BLK, ROWS)]
        for t, row in spots:
            parts.append((3, lambda t=t, row=row: weigh(t, row)))
        parts.append((1, middle))
        for t, row in spots:
            parts.append((1, lambda t=t, row=row: slope(t, row)))
        return parts

    def grad_parts(item, p):
        places = [place(pick) for pick in picks_of(item)]

        def keyed(t, part, row, size):
            slot, within = places[t]
            left, right = ((SG, QN), (D, DN))[part]
            start = t * BLK + row
            wide = low(t, row) if size <= SUB else 0
            add = dot(left[p][start:start + size, wide:], right[p][wide:, :])
            acc_ref[slot, part, pl.ds(within + row, size), :] += add
            return spread(add)

        def queried(lo, size):
            keys_t = jnp.concatenate([kt_ref[slot, :, pl.ds(within, BLK)] for slot, within in places], axis=1)
            part = dot(keys_t, SG[p][:, lo:lo + size])
            OUT[p][lo:lo + size, :] = (part * (INV[p][:, lo:lo + size] * (keep_gain * factor))).T
            return spread(part)

        parts = []
        for t in range(TOPK):
            for row in range(0, BLK, PIECE):
                parts.append(lambda t=t, row=row: keyed(t, 1, row, PIECE))
                parts.append(lambda t=t, row=row: keyed(t, 0, row, PIECE))
            if t % 2:
                parts.append(lambda t=t: queried(t // 2 * 2 * SUB, 2 * SUB))
        return parts

    def run(parts):
        for part in parts:
            part()

    def mix(soft, dots, ties):
        whole = sum(cost for cost, _ in soft)
        done, k = 0, 0
        held = []
        for cost, part in soft:
            while k < len(dots) and k * whole <= done * len(dots):
                held.append(dots[k]())
                k += 1
                if len(held) > LAG:
                    tie = held.pop(0)
                    if tie is not None:
                        ties[:] = [tie if not ties else ties[0] + tie]
            part()
            done += cost
        run(dots[k:])

    def weave(a, b):
        spots = [((i + 0.5) / len(a), 0, x) for i, x in enumerate(a)]
        spots += [((i + 0.5) / len(b), 1, x) for i, x in enumerate(b)]
        return [x for _, _, x in sorted(spots, key=lambda y: y[:2])]

    def send(item, p):
        rows, cols = where_of(item)
        return pltpu.make_async_copy(OUT[p], qg_ref.at[rows, cols], out_sem.at[p])

    @pl.when(pair == 0)
    def _():
        kv_col = pl.ds(pl.multiple_of(kv_column(), HD), HD)
        loads = [
            pltpu.make_async_copy(q_hbm, q_ref, load_sem.at[0]),
            pltpu.make_async_copy(do_hbm, do_ref, load_sem.at[1]),
            pltpu.make_async_copy(key_ref.at[:, kv_col], kv_ref.at[0, 0], load_sem.at[2]),
            pltpu.make_async_copy(value_ref.at[:, kv_col], kv_ref.at[0, 1], load_sem.at[3]),
            pltpu.make_async_copy(gathered_ref, kv_ref.at[pl.ds(1, window - 1)], load_sem.at[4]),
            pltpu.make_async_copy(bits_hbm, bits_ref, load_sem.at[5]),
        ]
        for load in loads:
            load.start()
        acc_ref[...] = jnp.zeros_like(acc_ref)
        for ref in D + SG:
            ref[...] = jnp.zeros_like(ref)
        QN[1][...] = jnp.zeros_like(QN[1])
        DN[1][...] = jnp.zeros_like(DN[1])
        INV[1][...] = jnp.zeros_like(INV[1])
        for load in loads:
            load.wait()
        for slot in range(window):
            kt_ref[slot] = kv_ref[slot, 0].T
        run(score_parts(0, 0))

    last = pl.num_programs(0) - 1
    for p in range(2):
        item = pair * 2 + p
        after = jnp.minimum(item + 1, steps - 1)
        before = jnp.maximum(item - 1, 0)
        target = jnp.where(item == 0, 1, item - 1)

        @pl.when(pair > 0)
        def _():
            send(jnp.maximum(target - 2, 0), 1 - p).wait()

        ties = []
        mix(soft_parts(item, p, ties), weave(score_parts(after, 1 - p), grad_parts(before, 1 - p)), ties)
        send(target, 1 - p).start()

    @pl.when(pair == last)
    def _():
        send(0, 1).wait()
        run(grad_parts(steps - 1, 1))
        send(steps - 1, 1).start()
        for part, scale in ((0, keep_gain * factor), (1, keep_gain)):
            own_ref[part] = acc_ref[0, part] * scale
            for slot in range(1, window):
                far_ref[slot - 1, part] = (acc_ref[slot, part] * scale).astype(jnp.bfloat16)
        send(0, 0).wait()
        send(0, 1).wait()


def kv_column():
    return lax.axis_index("head") * (HEADS // lax.axis_size("head")) // (HEADS // KVH) * HD


def block_grads(query, out_grad, key, value, gathered, bits, chosen, drop_seed):
    rows = query.shape[0]
    local_heads = query.shape[1] // HD
    local_blocks = rows // BLK
    window = gathered.shape[0] + 1
    steps = local_heads * local_blocks
    flops = steps * TOPK * 5 * 2 * BLK * BLK * HD
    kernel = lambda *refs: grads_kernel(local_blocks, window, steps, *refs)
    f32, bf16 = jnp.float32, jnp.bfloat16
    twice = lambda shape, dtype: [pltpu.VMEM(shape, dtype)] * 2
    return pl.pallas_call(
        kernel,
        name="block_grads",
        grid_spec=pltpu.PrefetchScalarGridSpec(
            num_scalar_prefetch=2,
            grid=(steps // 2,),
            in_specs=[pl.BlockSpec(memory_space=pl.ANY)] * 6,
            out_specs=[
                pl.BlockSpec(memory_space=pl.ANY),
                pl.BlockSpec((window - 1, 2, rows, HD), lambda i, *_: (0, 0, 0, 0)),
                pl.BlockSpec((2, rows, HD), lambda i, *_: (0, 0, 0)),
            ],
            scratch_shapes=twice((TOPK * BLK, BLK), f32) + twice((TOPK * BLK, BLK), f32)
            + twice((TOPK * BLK, BLK), bf16) + twice((TOPK * BLK, BLK), bf16)
            + twice((TOPK, 8, BLK), f32)
            + twice((HD, BLK), bf16) * 2 + twice((BLK, HD), bf16) * 2
            + twice((1, BLK), f32) + twice((BLK, HD), f32)
            + [
                pltpu.VMEM((window, 2, rows, HD), f32),
                pltpu.VMEM((window, HD, rows), bf16),
                pltpu.VMEM((window, 2, rows, HD), bf16),
                pltpu.VMEM(bits.shape, jnp.int32),
                pltpu.VMEM(query.shape, bf16),
                pltpu.VMEM(query.shape, bf16),
                pltpu.SemaphoreType.DMA((6,)),
                pltpu.SemaphoreType.DMA((2,)),
            ],
        ),
        out_shape=[
            jax.ShapeDtypeStruct((rows, local_heads * HD), f32),
            jax.ShapeDtypeStruct((window - 1, 2, rows, HD), bf16),
            jax.ShapeDtypeStruct((2, rows, HD), f32),
        ],
        compiler_params=pltpu.CompilerParams(vmem_limit_bytes=60 << 20),
        cost_estimate=pl.CostEstimate(flops=flops, bytes_accessed=20 << 20, transcendentals=steps * TOPK * BLK * BLK),
    )(chosen.reshape(-1), drop_seed, query, out_grad, key, value, gathered, bits)


def mask_rows(chosen_ref, seed_ref, bits_ref, steps, local_blocks, row, lo):
    shard = lax.axis_index("seq")
    size = 16
    at = (pl.ds(row, size), slice(0, BLK))
    place = ((lax.broadcasted_iota(jnp.int32, (size, BLK), 0) + row) * 9973
             + lax.broadcasted_iota(jnp.int32, (size, BLK), 1) * 40503)
    for word in range(bits_ref.shape[0]):
        held = jnp.zeros((size, BLK), jnp.int32)
        for j in range(32):
            item, t = (word * 32 + j) // TOPK, j % TOPK
            own = shard * local_blocks + item % local_blocks
            base = seed_ref[item // local_blocks] + own * (BLK * 40503) + chosen_ref[item * TOPK + t] * (BLK * 9973)
            cut = lo if t == 0 else 0
            bit = jnp.int32(1 << j if j < 31 else -(1 << 31))
            part = jnp.where(kept(place[:, cut:] + base), bit, 0)
            if cut:
                part = jnp.concatenate([jnp.zeros((size, cut), jnp.int32), part], axis=1)
            held = held | part
        bits_ref[(word,) + at] = held


def masks_kernel(steps, local_blocks, chosen_ref, seed_ref, bits_ref):
    @pl.loop(0, BLK // 16)
    def _(i):
        mask_rows(chosen_ref, seed_ref, bits_ref, steps, local_blocks, pl.multiple_of(i * 16, 16), 0)


def masks(chosen, drop_seed, local_blocks):
    steps = chosen.size // TOPK
    smem = pl.BlockSpec(memory_space=pltpu.SMEM)
    return pl.pallas_call(
        lambda *refs: masks_kernel(steps, local_blocks, *refs),
        name="masks",
        out_shape=jax.ShapeDtypeStruct((steps * TOPK // 32, BLK, BLK), jnp.int32),
        in_specs=[smem, smem],
        out_specs=pl.BlockSpec(memory_space=pltpu.VMEM),
    )(chosen.reshape(-1), drop_seed)


CHUNKS = 4


def seq_peer(by):
    size = lax.axis_size("seq")
    return {"seq": lax.rem(lax.axis_index("seq") + by + size, size)}


def meet(peers):
    barrier = pltpu.get_barrier_semaphore()
    for peer in peers:
        pl.semaphore_signal(barrier, inc=1, device_id=peer, device_id_type=pl.DeviceIdType.MESH)
    pl.semaphore_wait(barrier, len(peers))


def remote(src, dst, send, recv, peer):
    return pltpu.make_async_remote_copy(
        src_ref=src, dst_ref=dst, send_sem=send, recv_sem=recv, device_id=peer,
        device_id_type=pl.DeviceIdType.MESH,
    )


def gather_kernel(steps, local_blocks, chosen_ref, seed_ref, key_ref, value_ref, far_ref, bits_ref, send_sem, recv_sem):
    shard = lax.axis_index("seq")
    size = lax.axis_size("seq")
    odd = lax.rem(shard, 2)
    col = pl.ds(pl.multiple_of(lax.axis_index("head") * HD, HD), HD)
    half = key_ref.shape[0] // 2
    mate = {"seq": shard + 1 - 2 * odd}
    ahead = seq_peer(2)
    barrier = pltpu.get_barrier_semaphore()
    gives = shard < size - 2
    takes = shard >= 2
    relays = jnp.logical_and(odd == 0, jnp.logical_and(gives, takes))
    relayed = jnp.logical_and(odd == 0, shard >= 4)

    def greet(peer):
        pl.semaphore_signal(barrier, inc=1, device_id=peer, device_id_type=pl.DeviceIdType.MESH)

    for peer in (ahead, seq_peer(-2), mate):
        greet(peer)
    pl.semaphore_wait(barrier, 3)

    def own(c):
        return (key_ref, value_ref)[c // 2].at[pl.ds(c % 2 * half, half), col]

    def far(k, c):
        return far_ref.at[k, c // 2, pl.ds(c % 2 * half, half), :]

    def own_ahead(c):
        return remote(own(c), far(1, c), send_sem.at[0, c], recv_sem.at[1, c], ahead)

    def own_mate(c):
        return remote(own(c), far(0, c), send_sem.at[1, c], recv_sem.at[0, c], mate)

    def pass_mate(c, k):
        return remote(far(1, c), far(k, c), send_sem.at[2, c], recv_sem.at[k, c], mate)

    def pass_ahead(c):
        return remote(far(0, c), far(2, c), send_sem.at[3, c], recv_sem.at[2, c], ahead)

    for c in range(CHUNKS):
        @pl.when(gives)
        def _():
            own_ahead(c).start()

        @pl.when(odd == 0)
        def _():
            own_mate(c).start()

    def near_event(c):
        @pl.when(takes)
        def _():
            own_ahead(c).wait_recv()

            @pl.when(odd == 0)
            def _():
                pass_mate(c, 2).start()

            @pl.when(odd == 1)
            def _():
                pass_mate(c, 0).start()

    def far_event(c):
        @pl.when(relays)
        def _():
            own_mate(c).wait_recv()
            pass_ahead(c).start()

    events = [lambda c=c: near_event(c) for c in range(CHUNKS)] + [lambda c=c: far_event(c) for c in range(CHUNKS)]
    order = [0, 1, 4, 2, 5, 3, 6, 7]
    spots = MASK_SPOTS
    rows = 16
    loops = SUB // rows
    for c in range(BLK // SUB):
        @pl.loop(0, loops)
        def _(i):
            for spot, event in zip(spots, order):
                if spot // loops == c:
                    pl.when(i == spot % loops)(events[event])
            mask_rows(chosen_ref, seed_ref, bits_ref, steps, local_blocks,
                      pl.multiple_of(c * SUB + i * rows, rows), c * SUB)

    for c in range(CHUNKS):
        @pl.when(jnp.logical_and(odd == 0, takes))
        def _():
            pass_mate(c, 2).wait_send()

        @pl.when(jnp.logical_and(odd == 0, jnp.logical_and(takes, jnp.logical_not(gives))))
        def _():
            own_mate(c).wait_recv()

        @pl.when(odd == 0)
        def _():
            own_mate(c).wait_send()

        @pl.when(relayed)
        def _():
            pass_ahead(c).wait_recv()

        @pl.when(relays)
        def _():
            pass_ahead(c).wait_send()

        @pl.when(odd == 1)
        def _():
            own_mate(c).wait_recv()

        @pl.when(jnp.logical_and(odd == 1, takes))
        def _():
            remote(far(1, c), far(2, c), send_sem.at[2, c], recv_sem.at[2, c], mate).wait_recv()
            pass_mate(c, 0).wait_send()

        @pl.when(gives)
        def _():
            own_ahead(c).wait_send()


MASK_SPOTS = [11, 14, 15, 18, 19, 22, 23, 27]


def gather(key, value, chosen, drop_seed):
    rows = key.shape[0]
    steps = chosen.size // TOPK
    smem = pl.BlockSpec(memory_space=pltpu.SMEM)
    return pl.pallas_call(
        lambda *refs: gather_kernel(steps, rows // BLK, *refs),
        name="gather",
        out_shape=[
            jax.ShapeDtypeStruct((3, 2, rows, HD), jnp.bfloat16),
            jax.ShapeDtypeStruct((steps * TOPK // 32, BLK, BLK), jnp.int32),
        ],
        in_specs=[smem, smem] + [pl.BlockSpec(memory_space=pl.ANY)] * 2,
        out_specs=[pl.BlockSpec(memory_space=pl.ANY), pl.BlockSpec(memory_space=pltpu.VMEM)],
        scratch_shapes=[pltpu.SemaphoreType.DMA((4, CHUNKS)), pltpu.SemaphoreType.DMA((3, CHUNKS))],
        compiler_params=pltpu.CompilerParams(collective_id=0, has_side_effects=True, vmem_limit_bytes=60 << 20),
    )(chosen.reshape(-1), drop_seed, key, value)


def reduce_kernel(ranks, far_hbm, own_hbm, kg_ref, vg_ref, in_far, in_near, in_two, in_own, up_near, up_two,
                  in_head, up_head, total, far_ref, own_ref, send_sem, recv_sem, head_send, head_recv, load_sem):
    shard = lax.axis_index("seq")
    rank = lax.axis_index("head")
    odd = lax.rem(shard, 2)
    mate = {"seq": shard + 1 - 2 * odd}
    back = seq_peer(-2)
    others = [{"head": lax.rem(rank + d, ranks)} for d in range(1, ranks)]
    loads = [
        pltpu.make_async_copy(far_hbm.at[pl.ds(0, 2)], far_ref, load_sem.at[0]),
        pltpu.make_async_copy(own_hbm, own_ref, load_sem.at[1]),
    ]
    for load in loads:
        load.start()
    meet([back, seq_peer(2), mate] + others)
    piece = in_near.shape[2]

    def rows(c):
        return pl.ds(c * piece, piece)

    def far_back(c):
        return remote(far_hbm.at[2, :, rows(c)], in_far.at[c], send_sem.at[0, c], recv_sem.at[0, c], back)

    def own_mate(c):
        return remote(far_hbm.at[0, :, rows(c)], in_own.at[c], send_sem.at[0, c], recv_sem.at[1, c], mate)

    def far_mate(c):
        return remote(far_hbm.at[2, :, rows(c)], in_near.at[c], send_sem.at[1, c], recv_sem.at[2, c], mate)

    def near_mate(c):
        return remote(up_near.at[c], in_near.at[c], send_sem.at[1, c], recv_sem.at[2, c], mate)

    def two_back(c):
        return remote(up_two.at[c], in_two.at[c], send_sem.at[2, c], recv_sem.at[3, c], back)

    def to_head(c):
        return remote(up_head.at[c], in_head.at[rank], head_send.at[c], head_recv.at[rank], {"head": c})

    for c in range(ranks):
        @pl.when(odd == 0)
        def _():
            far_back(c).start()

        @pl.when(odd == 1)
        def _():
            far_mate(c).start()

    @pl.when(odd == 1)
    def _():
        for c in range(ranks):
            own_mate(c).start()

    def stage_near(c):
        @pl.when(odd == 0)
        def _():
            far_back(c).wait_recv()
            up_near[c] = (far_ref[0, :, rows(c)].astype(jnp.float32) + in_far[c].astype(jnp.float32)).astype(jnp.bfloat16)
            near_mate(c).start()

    def stage_two(c):
        near_mate(c).wait_recv()
        up_two[c] = (far_ref[1, :, rows(c)].astype(jnp.float32) + in_near[c].astype(jnp.float32)).astype(jnp.bfloat16)
        two_back(c).start()

    def stage_own(c):
        two_back(c).wait_recv()
        total[c] = own_ref[:, rows(c)] + in_two[c].astype(jnp.float32)

        @pl.when(odd == 0)
        def _():
            own_mate(c).wait_recv()
            total[c] += in_own[c].astype(jnp.float32)

        @pl.when(rank == c)
        def _():
            kg_ref[:, c * HD:(c + 1) * HD] = total[c, 0]
            vg_ref[:, c * HD:(c + 1) * HD] = total[c, 1]

        @pl.when(rank != c)
        def _():
            up_head[c] = total[c].astype(jnp.bfloat16)
            to_head(c).start()

    for load in loads:
        load.wait()
    for k in range(ranks + 2):
        if k < ranks:
            stage_near(k)
        if 0 <= k - 1 < ranks:
            stage_two(k - 1)
        if 0 <= k - 2:
            stage_own(k - 2)

    for c in range(ranks):
        @pl.when(rank != c)
        def _():
            remote(up_head.at[c], in_head.at[c], head_send.at[c], head_recv.at[c], {"head": c}).wait_recv()
            kg_ref[:, c * HD:(c + 1) * HD] = in_head[c, 0].astype(jnp.float32)
            vg_ref[:, c * HD:(c + 1) * HD] = in_head[c, 1].astype(jnp.float32)
            to_head(c).wait_send()

        two_back(c).wait_send()

        @pl.when(odd == 0)
        def _():
            far_back(c).wait_send()
            near_mate(c).wait_send()

        @pl.when(odd == 1)
        def _():
            own_mate(c).wait_send()
            far_mate(c).wait_send()


def reduce(far, own):
    ranks = lax.axis_size("head")
    rows = own.shape[1]
    piece = rows // ranks
    part = pltpu.VMEM((ranks, 2, piece, HD), jnp.bfloat16)
    return pl.pallas_call(
        lambda *refs: reduce_kernel(ranks, *refs),
        name="reduce",
        out_shape=[jax.ShapeDtypeStruct((piece, ranks * HD), jnp.float32)] * 2,
        in_specs=[pl.BlockSpec(memory_space=pl.ANY)] * 2,
        out_specs=[pl.BlockSpec(memory_space=pltpu.VMEM)] * 2,
        scratch_shapes=[part] * 8 + [
            pltpu.VMEM((ranks, 2, piece, HD), jnp.float32),
            pltpu.VMEM((2,) + far.shape[1:], jnp.bfloat16),
            pltpu.VMEM(own.shape, jnp.float32),
            pltpu.SemaphoreType.DMA((3, ranks)),
            pltpu.SemaphoreType.DMA((4, ranks)),
            pltpu.SemaphoreType.DMA((ranks,)),
            pltpu.SemaphoreType.DMA((ranks,)),
            pltpu.SemaphoreType.DMA((2,)),
        ],
        compiler_params=pltpu.CompilerParams(collective_id=1, has_side_effects=True, vmem_limit_bytes=60 << 20),
    )(far, own)


def local(query, key, value, out_grad, chosen, drop_seed):
    rows = query.shape[0]
    local_heads = query.shape[1] // HD
    size = lax.axis_size("seq")
    ranks = lax.axis_size("head")
    window = min(SPAN, size // 2)
    kv_col = kv_column()
    paired = window == 4 and ranks == KVH and size % 2 == 0
    if paired:
        gathered, bits = gather(key, value, chosen, drop_seed)
    else:
        bits = masks(chosen, drop_seed, rows // BLK)
        own_pair = jnp.stack(
            [
                lax.dynamic_slice_in_dim(key, kv_col, HD, 1),
                lax.dynamic_slice_in_dim(value, kv_col, HD, 1),
            ]
        )
        gathered = jnp.stack([shifted(own_pair, "seq", d) for d in range(1, window)])
    query_grad, far, own = block_grads(query, out_grad, key, value, gathered, bits, chosen, drop_seed)
    if paired:
        key_grad, value_grad = reduce(far, own)
        return (query_grad, key_grad, value_grad)
    for d in range(1, window):
        own = own + shifted(far[d - 1], "seq", -d).astype(jnp.float32)
    pieces = own.reshape(2, ranks, rows // ranks, HD)
    swapped = lax.all_to_all(pieces, "head", 1, 1, tiled=True)
    summed = swapped.reshape(2, KVH, ranks // KVH, rows // ranks, HD).sum(2)
    both = summed.transpose(0, 2, 1, 3).reshape(2, rows // ranks, KVH * HD)
    return (query_grad, both[0], both[1])


def solution(mesh):
    in_specs = (
        P("seq", "head"),
        P("seq", None),
        P("seq", None),
        P("seq", "head"),
        P("head", "seq", None),
        P("head"),
    )
    out_specs = (P("seq", "head"), P(("seq", "head"), None), P(("seq", "head"), None))
    return jax.shard_map(local, mesh=mesh, in_specs=in_specs, out_specs=out_specs, check_vma=False)
```
